32 devices in a mesh: ctx: 2 (over y), fsdp: 16 (over z, x, core).
Axes of the slice: x: 2, y: 2, z: 4, core: 2. Of those that a mesh axis runs over, the one named last changes fastest.
Arguments:
- block_in: bfloat16 [16, 512, 640], P('fsdp', 'ctx'), may hold values from -6 to 6
- positions: int32 [16, 512], P('fsdp', 'ctx'), may hold values from 0 to 511, as said below
- norm_gains: float32 [4, 640], replicated, may hold values from 0.25 to 1.75
- qk_gains: float32 [2, 256], replicated, may hold values from 0.5 to 4.5
- mat_query: bfloat16 [1024, 640], P('fsdp'), may hold values from -0.19764235 to 0.19764235
- mat_keyval: bfloat16 [512, 640], P('fsdp'), may hold values from -0.19764235 to 0.19764235
- mat_out: bfloat16 [1024, 640], P('fsdp'), may hold values from -0.1875 to 0.1875
- mat_gate: bfloat16 [2048, 640], P('fsdp'), may hold values from -0.25 to 0.25
- mat_up: bfloat16 [2048, 640], P('fsdp'), may hold values from -0.25 to 0.25
- mat_down: bfloat16 [2048, 640], P('fsdp'), may hold values from -0.125 to 0.125
- cotangent: bfloat16 [16, 512, 640], P('fsdp', 'ctx'), may hold values from -6 to 6
Outputs:
- block_out: bfloat16 [16, 512, 640], P('fsdp', 'ctx')
- grad_input: float32 [16, 512, 640], P('fsdp', 'ctx')
- grad_query: float32 [1024, 640], P('fsdp')
- grad_keyval: float32 [512, 640], P('fsdp')
- grad_out: float32 [1024, 640], P('fsdp')
- grad_gate: float32 [2048, 640], P('fsdp')
- grad_up: float32 [2048, 640], P('fsdp')
- grad_down: float32 [2048, 640], P('fsdp')
- grad_norms: float32 [4, 640], replicated
- grad_qk: float32 [2, 256], replicated
The draws below stay inside these ranges and needn't reach their ends.
Inputs may be any that keep to these rules, and one draw needn't show every extreme that they name: Each sequence holds every position 0 to 511 once, in runs of 128 consecutive ascending positions that start at multiples of 128; one device's 256 tokens of a sequence hold run b and run 4 - 1 - b, in either order.
All inputs are finite; a program needn't handle non-finite values.
Results may differ from the reference program's by a relative error of at most 0.02.
The reference program's roundings to bfloat16 on the way count: a program that leaves them out, or rounds other values in their place, can miss the bound.
Values may be sent and summed in bfloat16 or wider, within the bound.
No kernel may reach another device: no remote copies, remote signals or barrier semaphores. Data moves between devices by JAX's collectives and lax.ppermute only.
A program may use at most 128 MiB of HBM per device.

```python
import math
import jax
import jax.numpy as jnp
from jax import lax

D = 640
HEADS = 4
HD = 256
FF = 2048
RUN = 128
SEQ = 512
RUNS = 4
SEQS = 16


def weight_pair(key):
    base_key = jax.random.fold_in(key, 7)
    key_query, key_keyval = jax.random.split(base_key, 2)
    keyval = jax.random.truncated_normal(key_keyval, -4.0, 4.0, (2 * HD, D), jnp.float32) * D ** (-0.5)
    queries = jax.random.truncated_normal(key_query, -4.0, 4.0, (HEADS * HD, D), jnp.float32) * D ** (-0.5)
    return (queries, keyval)


def draw_mat_query(key, part):
    return weight_pair(key)[0].astype(jnp.bfloat16)


def draw_mat_keyval(key, part):
    return weight_pair(key)[1].astype(jnp.bfloat16)


def draw_qk_gains(key, part):
    gain_key = jax.random.fold_in(key, 19)
    return jax.random.uniform(gain_key, (2, HD), jnp.float32, 0.5, 1.5)


def order_one(single_key):
    return jax.random.permutation(single_key, RUNS // 2)


def draw_positions(key, part):
    key_order, key_flip = jax.random.split(jax.random.fold_in(key, 3))
    orders = jax.vmap(order_one)(jax.random.split(key_order, SEQS)).astype(jnp.int32)
    flips = jax.random.randint(key_flip, (SEQS, RUNS // 2), 0, 2)
    highs = RUNS - 1 - orders
    first_run = jnp.where(flips == 1, highs, orders)
    second_run = jnp.where(flips == 1, orders, highs)
    run_ids = jnp.stack([first_run, second_run], axis=-1)
    places = run_ids[..., None] * RUN + jnp.arange(RUN, dtype=jnp.int32)
    return places.reshape(SEQS, SEQ).astype(jnp.int32)


def block_scale(stream_key, shape, cuts, smallest, top_value):
    level = 1.0
    for position, shards_of in cuts:
        heights = jax.random.uniform(jax.random.fold_in(jax.random.fold_in(stream_key, 6), position), (shards_of,), jnp.float32, smallest / len(cuts), top_value / len(cuts))
        level = level * jnp.repeat(jnp.exp(heights), shape[position] // shards_of).reshape((-1,) + (1,) * (len(shape) - 1 - position))
    return level


def bell_draw(key, dims, spread, bound, cuts=(), kind=jnp.bfloat16):
    result = jax.random.normal(key, dims, jnp.float32) * spread
    if len(cuts) > 0:
        result = block_scale(key, dims, cuts, -0.22, 0.18) * result
    return jnp.clip(result, min=-bound, max=bound).astype(kind)


def setup_inputs(seed: int = 0) -> dict:
    keys = jax.random.split(jax.random.key(seed), 12)
    return {
        "block_in": bell_draw(keys[0], (SEQS, SEQ, D), 1.0, 6.0, ((0, 16), (1, 2))),
        "positions": draw_positions(jax.random.fold_in(keys[11], 71), 0),
        "norm_gains": jnp.clip(1.0 + 0.15 * jax.random.normal(keys[2], (4, D), jnp.float32), 0.25, 1.75),
        "qk_gains": draw_qk_gains(jax.random.fold_in(keys[11], 71), 0),
        "mat_query": draw_mat_query(jax.random.fold_in(keys[11], 71), 0),
        "mat_keyval": draw_mat_keyval(jax.random.fold_in(keys[11], 71), 0),
        "mat_out": bell_draw(keys[6], (HEADS * HD, D), (HEADS * HD) ** -0.5, 0.1875, ((0, 16),)),
        "mat_gate": bell_draw(keys[7], (FF, D), D ** -0.5, 0.25, ((0, 16),)),
        "mat_up": bell_draw(keys[8], (FF, D), D ** -0.5, 0.25, ((0, 16),)),
        "mat_down": bell_draw(keys[9], (FF, D), FF ** -0.5, 0.125, ((0, 16),)),
        "cotangent": bell_draw(keys[10], (SEQS, SEQ, D), 1.0, 6.0, ((0, 16), (1, 2))),
    }


EPS = 1e-06
ROPE_BASE = 1000000.0
NEG_FILL = -1e+30

def rms_norm(vector, gains):
    return vector * lax.rsqrt(lax.optimization_barrier(jnp.mean(vector * vector, axis=-1, keepdims=True)) + EPS) * gains

def rope_tables(places, width):
    half_width = width // 2
    frequency = jnp.exp(jnp.arange(half_width, dtype=jnp.float32) * (-2.0 * math.log(ROPE_BASE) / width))
    angles = places.astype(jnp.float32)[:, None] * frequency[None, :]
    return (jnp.cos(angles), jnp.sin(angles))

def rotate(vector, cosines, sine_table):
    half_width = vector.shape[-1] // 2
    first_half = vector[..., :half_width]
    second_half = vector[..., half_width:]
    return jnp.concatenate([first_half * cosines - second_half * sine_table, second_half * cosines + first_half * sine_table], axis=-1)

def unrotate(vector, cosines, sine_table):
    half_width = vector.shape[-1] // 2
    first_half = vector[..., :half_width]
    second_half = vector[..., half_width:]
    return jnp.concatenate([first_half * cosines + second_half * sine_table, second_half * cosines - first_half * sine_table], axis=-1)

def product(left, right):
    return jnp.dot(left, right, preferred_element_type=jnp.float32)

def times_transposed(left, right):
    return lax.dot_general(left, right, (((1,), (1,)), ((), ())), preferred_element_type=jnp.float32)

def transposed_times(left, right):
    return lax.dot_general(left, right, (((0,), (0,)), ((), ())), preferred_element_type=jnp.float32)

def gelu_gate(gate_proj, up_proj):
    return jax.nn.gelu(gate_proj, approximate=True) * up_proj

def widen(array):
    return array.astype(jnp.float32)

def attend_forward(query_rot, key_rot, value_rows, query_places, key_places, score_scale):
    scores = jnp.einsum('lhd,md->hlm', widen(query_rot), widen(key_rot)) * score_scale
    allowed = key_places[None, None, :] <= query_places[None, :, None]
    row_best = lax.optimization_barrier(jnp.max(jnp.where(allowed, scores, NEG_FILL), axis=-1))
    probability = jnp.where(allowed, jnp.exp(scores - row_best[..., None]), 0.0)
    row_total = lax.optimization_barrier(jnp.sum(probability, axis=-1))
    mixing = jnp.einsum('hlm,md->lhd', widen(probability.astype(jnp.bfloat16)), widen(value_rows)) / row_total.T[..., None]
    return (mixing, row_best + jnp.log(row_total))

def attend_backward(query_rot, key_rot, value_rows, query_places, key_places, score_scale, mixing, log_total, d_mixing_b):
    scores = jnp.einsum('lhd,md->hlm', widen(query_rot), widen(key_rot)) * score_scale
    allowed = key_places[None, None, :] <= query_places[None, :, None]
    probability = jnp.where(allowed, jnp.exp(scores - log_total[..., None]), 0.0)
    delta = lax.optimization_barrier(jnp.sum(widen(d_mixing_b) * mixing, axis=-1)).T
    d_prob = jnp.einsum('lhd,md->hlm', widen(d_mixing_b), widen(value_rows))
    d_scores_b = (probability * (d_prob - delta[..., None]) * score_scale).astype(jnp.bfloat16)
    d_query_rot = jnp.einsum('hlm,md->lhd', widen(d_scores_b), widen(key_rot))
    d_key_rot = jnp.einsum('hlm,lhd->md', widen(d_scores_b), widen(query_rot))
    d_value = jnp.einsum('hlm,lhd->md', widen(probability.astype(jnp.bfloat16)), widen(d_mixing_b))
    return (d_query_rot, d_key_rot, d_value)

def sequence_pass(block_row, place_row, cot_row, norm_gains, qk_gains, mats):
    full_query, full_keyval, full_out, full_gate, full_up, full_down = mats
    stream = block_row.astype(jnp.float32)
    row_count = stream.shape[0]
    head_dim = qk_gains.shape[1]
    head_count = full_query.shape[0] // head_dim
    score_scale = head_dim ** (-0.5)
    normed_in = rms_norm(stream, norm_gains[0]).astype(jnp.bfloat16)
    queries = times_transposed(normed_in, full_query).reshape(row_count, head_count, head_dim)
    key_values = times_transposed(normed_in, full_keyval)
    key_raw = key_values[:, :head_dim]
    cosines, sine_table = rope_tables(place_row, head_dim)
    query_rot = rotate(rms_norm(queries, qk_gains[0]), cosines[:, None, :], sine_table[:, None, :]).astype(jnp.bfloat16)
    key_rot = rotate(rms_norm(key_raw, qk_gains[1]), cosines, sine_table).astype(jnp.bfloat16)
    value_rows = key_values[:, head_dim:].astype(jnp.bfloat16)
    mixing, log_total = attend_forward(query_rot, key_rot, value_rows, place_row, place_row, score_scale)
    mixing_b = mixing.reshape(row_count, head_count * head_dim).astype(jnp.bfloat16)
    attend_out = product(mixing_b, full_out)
    resid = stream + rms_norm(attend_out, norm_gains[1])
    normed_mid = rms_norm(resid, norm_gains[2]).astype(jnp.bfloat16)
    gate_proj = times_transposed(normed_mid, full_gate)
    up_proj = times_transposed(normed_mid, full_up)
    hidden = gelu_gate(gate_proj, up_proj).astype(jnp.bfloat16)
    ffn_out = product(hidden, full_down)
    block_out = (resid + rms_norm(ffn_out, norm_gains[3])).astype(jnp.bfloat16)
    cot_full = cot_row.astype(jnp.float32)
    unused, ffn_back = jax.vjp(rms_norm, ffn_out, norm_gains[3])
    d_ffn, d_gain_three = ffn_back(cot_full)
    d_ffn_b = d_ffn.astype(jnp.bfloat16)
    d_hidden = times_transposed(d_ffn_b, full_down)
    grad_down = transposed_times(hidden, d_ffn_b)
    unused, gate_back = jax.vjp(gelu_gate, gate_proj, up_proj)
    d_gate, d_up = gate_back(d_hidden)
    d_gate_b = d_gate.astype(jnp.bfloat16)
    d_up_b = d_up.astype(jnp.bfloat16)
    d_mid = product(d_gate_b, full_gate) + product(d_up_b, full_up)
    grad_gate = transposed_times(d_gate_b, normed_mid)
    grad_up = transposed_times(d_up_b, normed_mid)
    unused, mid_back = jax.vjp(rms_norm, resid, norm_gains[2])
    d_resid_mid, d_gain_two = mid_back(d_mid)
    d_resid = cot_full + d_resid_mid
    unused, attend_back = jax.vjp(rms_norm, attend_out, norm_gains[1])
    d_attend, d_gain_one = attend_back(d_resid)
    d_attend_b = d_attend.astype(jnp.bfloat16)
    d_mixing_b = times_transposed(d_attend_b, full_out).reshape(row_count, head_count, head_dim).astype(jnp.bfloat16)
    grad_out = transposed_times(mixing_b, d_attend_b)
    d_query_rot, d_key_rot, d_value = attend_backward(query_rot, key_rot, value_rows, place_row, place_row, score_scale, mixing, log_total, d_mixing_b)
    d_query_norm = unrotate(d_query_rot, cosines[:, None, :], sine_table[:, None, :])
    d_key_norm = unrotate(d_key_rot, cosines, sine_table)
    unused, query_back = jax.vjp(rms_norm, queries, qk_gains[0])
    d_queries, d_gain_query = query_back(d_query_norm)
    unused, key_back = jax.vjp(rms_norm, key_raw, qk_gains[1])
    d_keys, d_gain_key = key_back(d_key_norm)
    d_query_b = d_queries.reshape(row_count, head_count * head_dim).astype(jnp.bfloat16)
    d_keyval_b = jnp.concatenate([d_keys, d_value], axis=1).astype(jnp.bfloat16)
    d_in = product(d_query_b, full_query) + product(d_keyval_b, full_keyval)
    grad_query = transposed_times(d_query_b, normed_in)
    grad_keyval = transposed_times(d_keyval_b, normed_in)
    unused, in_back = jax.vjp(rms_norm, stream, norm_gains[0])
    d_stream, d_gain_zero = in_back(d_in)
    grad_input = d_resid + d_stream
    grads = (grad_query, grad_keyval, grad_out, grad_gate, grad_up, grad_down)
    grad_norms = jnp.stack([d_gain_zero, d_gain_one, d_gain_two, d_gain_three])
    grad_qk = jnp.stack([d_gain_query, d_gain_key])
    return (block_out, grad_input, grads, grad_norms, grad_qk)

def reference(block_in, positions, norm_gains, qk_gains, mat_query, mat_keyval, mat_out, mat_gate, mat_up, mat_down, cotangent):
    mats = (mat_query, mat_keyval, mat_out, mat_gate, mat_up, mat_down)

    def one_sequence(state_in, items):
        block_row, place_row, cot_row = items
        block_out, grad_input, grads, grad_norms, grad_qk = sequence_pass(block_row, place_row, cot_row, norm_gains, qk_gains, mats)
        summed = tuple((total + extra for total, extra in zip(state_in, grads + (grad_norms, grad_qk))))
        return (summed, (block_out, grad_input))
    init_state = tuple((jnp.zeros(matrix.shape, jnp.float32) for matrix in mats)) + (jnp.zeros(norm_gains.shape, jnp.float32), jnp.zeros(qk_gains.shape, jnp.float32))
    summed, stacked = lax.scan(one_sequence, init_state, (block_in, positions, cotangent))
    return (stacked[0], stacked[1], summed[0], summed[1], summed[2], summed[3], summed[4], summed[5], summed[6], summed[7])
```

```python
import functools
import math

import jax
import jax.numpy as jnp
from jax import lax
from jax.experimental import pallas as pl
from jax.experimental.pallas import tpu as pltpu
from jax.sharding import PartitionSpec as P


EPS = 1e-06
ROPE_BASE = 1000000.0
NEG_FILL = -1e30


def rms_norm(vector, gains):
    return vector * lax.rsqrt(jnp.mean(vector * vector, axis=-1, keepdims=True) + EPS) * gains


def rope_tables(places, width):
    half_width = width // 2
    frequency = jnp.exp(
        jnp.arange(half_width, dtype=jnp.float32) * (-2.0 * math.log(ROPE_BASE) / width)
    )
    angles = places.astype(jnp.float32)[:, None] * frequency[None, :]
    return (jnp.cos(angles), jnp.sin(angles))


def rotate(vector, cosines, sine_table):
    half_width = vector.shape[-1] // 2
    first_half = vector[..., :half_width]
    second_half = vector[..., half_width:]
    return jnp.concatenate(
        [
            first_half * cosines - second_half * sine_table,
            second_half * cosines + first_half * sine_table,
        ],
        axis=-1,
    )


def unrotate(vector, cosines, sine_table):
    half_width = vector.shape[-1] // 2
    first_half = vector[..., :half_width]
    second_half = vector[..., half_width:]
    return jnp.concatenate(
        [
            first_half * cosines + second_half * sine_table,
            second_half * cosines - first_half * sine_table,
        ],
        axis=-1,
    )


def product(left, right):
    return jnp.dot(left, right, preferred_element_type=jnp.float32)


def times_transposed(left, right):
    return lax.dot_general(
        left, right, (((1,), (1,)), ((), ())), preferred_element_type=jnp.float32
    )


def transposed_times(left, right):
    return lax.dot_general(
        left, right, (((0,), (0,)), ((), ())), preferred_element_type=jnp.float32
    )


def gelu_gate(gate_proj, up_proj):
    return jax.nn.gelu(gate_proj, approximate=True) * up_proj


def attend_backward(
    query_flat,
    key_rot,
    value_rows,
    query_places,
    key_places,
    score_scale,
    mixing_flat,
    log_total,
    d_mixing_flat,
):
    scores = times_transposed(query_flat, key_rot) * score_scale
    allowed = key_places[None, :] <= query_places[:, None]
    probability = jnp.where(allowed, jnp.exp(scores - log_total[:, None]), 0.0)
    delta = jnp.sum(d_mixing_flat.astype(jnp.float32) * mixing_flat, axis=-1)
    d_prob = times_transposed(d_mixing_flat, value_rows)
    d_scores_b = (probability * (d_prob - delta[:, None]) * score_scale).astype(jnp.bfloat16)
    d_query_rot = product(d_scores_b, key_rot)
    d_key_rot = transposed_times(d_scores_b, query_flat)
    d_value = transposed_times(probability.astype(jnp.bfloat16), d_mixing_flat)
    return (d_query_rot, d_key_rot, d_value)


def add_b(left, right):
    return (left.astype(jnp.float32) + right.astype(jnp.float32)).astype(jnp.bfloat16)


def assemble(pieces, moves, table, rows):
    width = pieces[0].shape[1]

    def body(table_ref, *refs):
        piece_refs = refs[: len(pieces)]
        out_refs = refs[len(pieces) : len(pieces) + len(rows)]
        sems = refs[-1]
        started = []
        for number, (piece, source, count, out, step, offset, entry) in enumerate(moves):
            start = pl.multiple_of(table_ref[entry] * step + offset, 16)
            copy = pltpu.make_async_copy(
                piece_refs[piece].at[pl.ds(source, count)],
                out_refs[out].at[pl.ds(start, count)],
                sems.at[number],
            )
            copy.start()
            started.append(copy)
        for copy in started:
            copy.wait()

    anywhere = pl.BlockSpec(memory_space=pl.ANY)
    return pl.pallas_call(
        body,
        out_shape=[jax.ShapeDtypeStruct((count, width), pieces[0].dtype) for count in rows],
        in_specs=[pl.BlockSpec(memory_space=pltpu.SMEM)] + [anywhere] * len(pieces),
        out_specs=[pl.BlockSpec(memory_space=pltpu.VMEM)] * len(rows),
        scratch_shapes=[pltpu.SemaphoreType.DMA((len(moves),))],
        name="assemble",
    )(table, *pieces)


class Links:
    def __init__(self, fsdp_size):
        self.size = fsdp_size
        self.bits = fsdp_size.bit_length() - 1
        self.deep = fsdp_size // 4
        self.chips = fsdp_size // 2
        self.ring = self.chips == 8
        self.index = lax.axis_index("fsdp")
        self.side = lax.axis_index("ctx")

    def across(self, array, bit):
        return lax.ppermute(array, "fsdp", [(i, i ^ (1 << bit)) for i in range(self.size)])

    def to_side(self, array):
        return lax.ppermute(array, "ctx", [(0, 1), (1, 0)])

    def by_side(self, here, there):
        return jnp.where(self.side == 0, here, there)

    def device_at(self, place, core):
        column = place // self.deep
        level = place % self.deep
        level = level + column * (self.deep - 1 - 2 * level)
        return level * 4 + column * 2 + core

    def place(self):
        column = (self.index // 2) % 2
        level = self.index // 4
        return level + column * (self.chips - 1 - 2 * level)

    def turned(self, array, step):
        pairs = [
            (
                self.device_at(place, core),
                self.device_at((place + step) % self.chips, core),
            )
            for place in range(self.chips)
            for core in range(2)
        ]
        return lax.ppermute(array, "fsdp", pairs)

    def order(self, shard):
        relative = shard ^ self.index
        found = relative * 0
        for bit in range(self.bits):
            found = found * 2 + ((relative >> bit) & 1)
        return found

    def gather(self, mats, relative):
        counts = [mat.shape[0] for mat in mats]
        shard = jnp.concatenate(mats)
        total = shard.shape[0]
        half = total // 2
        far = self.chips // 2
        pieces = [(shard, 0, 0)]
        ahead, behind = shard, shard
        for distance in range(1, far):
            ahead = self.turned(ahead, 1)
            behind = self.turned(behind, -1)
            pieces += [(ahead, -distance, 0), (behind, distance, 0)]
        pieces += [
            (self.turned(ahead[:half], 1), -far, 0),
            (self.turned(behind[half:], -1), far, half),
        ]
        arrays, moves, entries = [], [], []
        for other in range(2):
            for array, distance, first in pieces:
                owner = self.device_at(
                    (self.place() + distance) % self.chips, (self.index % 2) ^ other
                )
                number = len(arrays)
                arrays.append(self.across(array, 0) if other else array)
                entries.append(self.order(owner) if relative else owner)
                begin = 0
                for out, count in enumerate(counts):
                    low = max(begin, first)
                    high = min(begin + count, first + array.shape[0])
                    if low < high:
                        moves.append((number, low - first, high - low, out, count, low - begin, number))
                    begin += count
        table = jnp.stack(entries).astype(jnp.int32)
        return assemble(arrays, moves, table, [count * self.size for count in counts])

    def split(self, array, bit, relative):
        if relative:
            half = array.shape[0] // 2
            return array[:half], array[half:]
        own = (self.index >> bit) & 1
        axis = array.ndim - 3
        return (
            lax.dynamic_index_in_dim(array, own, axis, keepdims=False),
            lax.dynamic_index_in_dim(array, 1 - own, axis, keepdims=False),
        )

    def fold(self, terms, first_bit, relative):
        for bit in range(first_bit, self.bits):
            parts = [self.split(term, bit, relative) for term in terms]
            leaving = total_of([part[1] for part in parts]).astype(jnp.bfloat16)
            terms = [part[0] for part in parts] + [self.across(leaving, bit)]
        return total_of(terms)

    def blocks(self, array, relative):
        if relative:
            return array
        return array.reshape((2,) * self.bits + (-1, array.shape[-1]))

    def sum_all(self, array):
        for bit in range(self.bits):
            array = array + self.across(array, bit)
        return array + self.to_side(array)


def total_of(terms):
    total = terms[0].astype(jnp.float32)
    for term in terms[1:]:
        total = total + term.astype(jnp.float32)
    return total


def per_device(
    block_in,
    positions,
    norm_gains,
    qk_gains,
    mat_query,
    mat_keyval,
    mat_out,
    mat_gate,
    mat_up,
    mat_down,
    cotangent,
    *,
    fsdp_size,
):
    stream = block_in[0].astype(jnp.float32)
    places = positions[0]
    row_count = stream.shape[0]
    run_len = row_count // 2
    head_dim = qk_gains.shape[1]
    score_scale = head_dim ** (-0.5)
    links = Links(fsdp_size)
    side = links.side
    other_places = lax.ppermute(positions, "ctx", [(0, 1), (1, 0)])[0]
    relative = links.ring
    if links.ring:
        full_query, full_keyval, full_out = links.gather((mat_query, mat_keyval, mat_out), False)
        full_gate, full_up, full_down = links.gather((mat_gate, mat_up, mat_down), True)
    else:
        full_query, full_keyval, full_out, full_gate, full_up, full_down = [
            lax.all_gather(mat, "fsdp", axis=0, tiled=True)
            for mat in (mat_query, mat_keyval, mat_out, mat_gate, mat_up, mat_down)
        ]
    head_count = full_query.shape[0] // head_dim
    flat_rows = row_count * head_count
    normed_in = rms_norm(stream, norm_gains[0]).astype(jnp.bfloat16)
    queries = times_transposed(normed_in, full_query).reshape(row_count, head_count, head_dim)
    key_values = times_transposed(normed_in, full_keyval)
    key_raw = key_values[:, :head_dim]
    cosines, sine_table = rope_tables(places, head_dim)
    query_rot = rotate(
        rms_norm(queries, qk_gains[0]), cosines[:, None, :], sine_table[:, None, :]
    ).astype(jnp.bfloat16)
    query_flat = query_rot.reshape(flat_rows, head_dim)
    flat_places = jnp.repeat(places, head_count)
    key_rot = rotate(rms_norm(key_raw, qk_gains[1]), cosines, sine_table).astype(jnp.bfloat16)
    value_rows = key_values[:, head_dim:].astype(jnp.bfloat16)
    row_best = jnp.full((flat_rows,), NEG_FILL, jnp.float32)
    both_b = jnp.concatenate([key_rot, value_rows], axis=1)
    other_both = links.to_side(both_b)
    key_rows = jnp.concatenate([key_rot, other_both[:, :head_dim]], axis=0)
    value_piece = jnp.concatenate([value_rows, other_both[:, head_dim:]], axis=0)
    key_places = jnp.concatenate([places, other_places])
    scores = times_transposed(query_flat, key_rows) * score_scale
    allowed = key_places[None, :] <= flat_places[:, None]
    fresh_best = jnp.maximum(row_best, jnp.max(jnp.where(allowed, scores, NEG_FILL), axis=-1))
    probability = jnp.where(allowed, jnp.exp(scores - fresh_best[:, None]), 0.0)
    row_total = jnp.sum(probability, axis=-1)
    weighted = product(probability.astype(jnp.bfloat16), value_piece)
    row_best, row_total, weighted = (fresh_best, row_total, weighted)
    mixing_flat = weighted / row_total[:, None]
    log_total = row_best + jnp.log(row_total)
    mixing_b = mixing_flat.reshape(row_count, head_count * head_dim).astype(jnp.bfloat16)
    attend_out = product(mixing_b, full_out)
    resid = stream + rms_norm(attend_out, norm_gains[1])
    normed_mid = rms_norm(resid, norm_gains[2]).astype(jnp.bfloat16)
    gate_proj = times_transposed(normed_mid, full_gate)
    up_proj = times_transposed(normed_mid, full_up)
    hidden = gelu_gate(gate_proj, up_proj).astype(jnp.bfloat16)
    ffn_out = product(hidden, full_down)
    block_out = (resid + rms_norm(ffn_out, norm_gains[3])).astype(jnp.bfloat16)
    cot_full = cotangent[0].astype(jnp.float32)
    unused, ffn_back = jax.vjp(rms_norm, ffn_out, norm_gains[3])
    d_ffn, d_gain_three = ffn_back(cot_full)
    d_ffn_b = d_ffn.astype(jnp.bfloat16)
    d_hidden = times_transposed(d_ffn_b, full_down)

    def over_cores(rows, columns):
        if relative:
            half = rows.shape[1] // 2
            leaving = transposed_times(rows[:, half:], columns).astype(jnp.bfloat16)
            staying = transposed_times(rows[:, :half], columns).astype(jnp.bfloat16)
        else:
            product_b = transposed_times(rows, columns).astype(jnp.bfloat16)
            staying, leaving = links.split(links.blocks(product_b, relative), 0, relative)
        return [staying, links.across(leaving, 0)]

    def both_sides(total):
        total_b = total.astype(jnp.bfloat16)
        return total_b.astype(jnp.float32) + links.to_side(total_b).astype(jnp.float32)

    shard_down = both_sides(links.fold(over_cores(hidden, d_ffn_b), 1, relative))
    unused, gate_back = jax.vjp(gelu_gate, gate_proj, up_proj)
    d_gate, d_up = gate_back(d_hidden)
    d_gate_b = d_gate.astype(jnp.bfloat16)
    d_up_b = d_up.astype(jnp.bfloat16)
    d_first = links.by_side(d_gate_b, d_up_b)
    d_second = links.by_side(d_up_b, d_gate_b)
    second_sum = total_of(over_cores(d_second, normed_mid)).astype(jnp.bfloat16)
    first_terms = [links.to_side(second_sum)] + over_cores(d_first, normed_mid)
    first_sum = links.fold(first_terms, 1, relative).astype(jnp.bfloat16)
    second_sum = links.to_side(first_sum)
    shard_gate = links.by_side(first_sum, second_sum).astype(jnp.float32)
    shard_up = links.by_side(second_sum, first_sum).astype(jnp.float32)
    d_mid = product(d_gate_b, full_gate) + product(d_up_b, full_up)
    unused, mid_back = jax.vjp(rms_norm, resid, norm_gains[2])
    d_resid_mid, d_gain_two = mid_back(d_mid)
    d_resid = cot_full + d_resid_mid
    unused, attend_back = jax.vjp(rms_norm, attend_out, norm_gains[1])
    d_attend, d_gain_one = attend_back(d_resid)
    d_attend_b = d_attend.astype(jnp.bfloat16)
    d_mixing_flat = (
        times_transposed(d_attend_b, full_out).reshape(flat_rows, head_dim).astype(jnp.bfloat16)
    )

    def blocks_of(rows, columns):
        return links.blocks(transposed_times(rows, columns).astype(jnp.bfloat16), False)

    shard_out = both_sides(links.fold([blocks_of(mixing_b, d_attend_b)], 0, False))
    d_query_flat, d_key_all, d_value_all = attend_backward(
        query_flat,
        key_rows,
        value_piece,
        flat_places,
        key_places,
        score_scale,
        mixing_flat,
        log_total,
        d_mixing_flat,
    )
    key_back = jnp.concatenate(
        [d_key_all[row_count:], d_value_all[row_count:]], axis=1
    ).astype(jnp.bfloat16)
    key_back = links.to_side(key_back).astype(jnp.float32)
    d_key_rot = d_key_all[:row_count] + key_back[:, :head_dim]
    d_value = d_value_all[:row_count] + key_back[:, head_dim:]
    d_query_rot = d_query_flat.reshape(row_count, head_count, head_dim)
    d_query_norm = unrotate(d_query_rot, cosines[:, None, :], sine_table[:, None, :])
    d_key_norm = unrotate(d_key_rot, cosines, sine_table)
    unused, query_back = jax.vjp(rms_norm, queries, qk_gains[0])
    d_queries, d_gain_query = query_back(d_query_norm)
    unused, key_vjp = jax.vjp(rms_norm, key_raw, qk_gains[1])
    d_keys, d_gain_key = key_vjp(d_key_norm)
    d_query_b = d_queries.reshape(row_count, head_count * head_dim).astype(jnp.bfloat16)
    d_keyval_b = jnp.concatenate([d_keys, d_value], axis=1).astype(jnp.bfloat16)
    d_in = product(d_query_b, full_query) + product(d_keyval_b, full_keyval)
    tower = jnp.concatenate(
        [blocks_of(d_query_b, normed_in), blocks_of(d_keyval_b, normed_in)], axis=-2
    )
    tower = both_sides(links.fold([tower], 0, False))
    shard_query = tower[: mat_query.shape[0]]
    shard_keyval = tower[mat_query.shape[0] :]
    unused, in_back = jax.vjp(rms_norm, stream, norm_gains[0])
    d_stream, d_gain_zero = in_back(d_in)
    grad_input = d_resid + d_stream
    gains = jnp.concatenate(
        [d_gain_zero, d_gain_one, d_gain_two, d_gain_three, d_gain_query, d_gain_key]
    ).reshape(-1, 128)
    gains = links.sum_all(gains).reshape(-1)
    grad_norms = gains[: norm_gains.size].reshape(norm_gains.shape)
    grad_qk = gains[norm_gains.size :].reshape(qk_gains.shape)
    return (
        block_out[None],
        grad_input[None],
        shard_query,
        shard_keyval,
        shard_out,
        shard_gate,
        shard_up,
        shard_down,
        grad_norms,
        grad_qk,
    )


def solution(mesh):
    return jax.shard_map(
        functools.partial(per_device, fsdp_size=mesh.shape["fsdp"]),
        mesh=mesh,
        in_specs=(
            P("fsdp", "ctx", None),
            P("fsdp", "ctx"),
            P(),
            P(),
            P("fsdp", None),
            P("fsdp", None),
            P("fsdp", None),
            P("fsdp", None),
            P("fsdp", None),
            P("fsdp", None),
            P("fsdp", "ctx", None),
        ),
        out_specs=(
            P("fsdp", "ctx", None),
            P("fsdp", "ctx", None),
            P("fsdp", None),
            P("fsdp", None),
            P("fsdp", None),
            P("fsdp", None),
            P("fsdp", None),
            P("fsdp", None),
            P(),
            P(),
        ),
        check_vma=False,
    )
```

```python
import functools
import math

import jax
import jax.numpy as jnp
from jax import lax
from jax.experimental import pallas as pl
from jax.experimental.pallas import tpu as pltpu
from jax.sharding import PartitionSpec as P


EPS = 1e-06
ROPE_BASE = 1000000.0
NEG_FILL = -1e30


def rms_norm(vector, gains):
    return vector * lax.rsqrt(jnp.mean(vector * vector, axis=-1, keepdims=True) + EPS) * gains


def rope_tables(places, width):
    half_width = width // 2
    frequency = jnp.exp(
        jnp.arange(half_width, dtype=jnp.float32) * (-2.0 * math.log(ROPE_BASE) / width)
    )
    angles = places.astype(jnp.float32)[:, None] * frequency[None, :]
    return (jnp.cos(angles), jnp.sin(angles))


def rotate(vector, cosines, sine_table):
    half_width = vector.shape[-1] // 2
    first_half = vector[..., :half_width]
    second_half = vector[..., half_width:]
    return jnp.concatenate(
        [
            first_half * cosines - second_half * sine_table,
            second_half * cosines + first_half * sine_table,
        ],
        axis=-1,
    )


def product(left, right):
    return jnp.dot(left, right, preferred_element_type=jnp.float32)


def times_transposed(left, right):
    return lax.dot_general(
        left, right, (((1,), (1,)), ((), ())), preferred_element_type=jnp.float32
    )


def transposed_times(left, right):
    return lax.dot_general(
        left, right, (((0,), (0,)), ((), ())), preferred_element_type=jnp.float32
    )


def gelu_gate(gate_proj, up_proj):
    return jax.nn.gelu(gate_proj, approximate=True) * up_proj


def norm_back(vector, gains, cot):
    inverse = lax.rsqrt(jnp.mean(vector * vector, axis=-1, keepdims=True) + EPS)
    unit = vector * inverse
    scaled = cot * gains
    d_vector = inverse * (scaled - unit * jnp.mean(scaled * unit, axis=-1, keepdims=True))
    return d_vector, cot * unit


def attend_body(
    query_ref,
    own_ref,
    other_ref,
    place_ref,
    own_place_ref,
    other_place_ref,
    out_ref,
    stream_ref,
    gain_ref,
    mixing_ref,
    mixing_b_ref,
    log_ref,
    attend_ref,
    resid_ref,
    mid_ref,
    *,
    head_dim,
):
    rows, width = query_ref.shape
    score_scale = head_dim ** (-0.5)
    sources = (
        (own_ref, own_place_ref[...] <= place_ref[...]),
        (other_ref, other_place_ref[...] <= place_ref[...]),
    )
    for start in range(0, width, head_dim):
        query = query_ref[:, start : start + head_dim]
        scores = [
            jnp.where(
                allowed, times_transposed(query, both_ref[:, :head_dim]) * score_scale, NEG_FILL
            )
            for both_ref, allowed in sources
        ]
        best = jnp.maximum(
            jnp.max(scores[0], axis=-1, keepdims=True), jnp.max(scores[1], axis=-1, keepdims=True)
        )
        total = jnp.zeros((rows, 1), jnp.float32)
        weighted = jnp.zeros((rows, head_dim), jnp.float32)
        for (both_ref, allowed), score in zip(sources, scores):
            weights = jnp.where(allowed, jnp.exp(score - best), 0.0)
            total = total + jnp.sum(weights, axis=-1, keepdims=True)
            weighted = weighted + product(weights.astype(jnp.bfloat16), both_ref[:, head_dim:])
        mixing = weighted / total
        mixing_ref[:, start : start + head_dim] = mixing
        mixing_b_ref[:, start : start + head_dim] = mixing.astype(jnp.bfloat16)
        head = start // head_dim
        log_ref[:, head : head + 1] = best + jnp.log(total)
    attend = product(mixing_b_ref[...], out_ref[...])
    attend_ref[...] = attend
    resid = stream_ref[...].astype(jnp.float32) + rms_norm(attend, gain_ref[1:2, :])
    resid_ref[...] = resid
    mid_ref[...] = rms_norm(resid, gain_ref[2:3, :]).astype(jnp.bfloat16)


def attend_back_body(
    d_attend_ref,
    out_ref,
    query_ref,
    own_ref,
    other_ref,
    place_ref,
    own_place_ref,
    other_place_ref,
    mixing_ref,
    log_ref,
    raw_ref,
    cosine_ref,
    sine_ref,
    gain_ref,
    d_query_ref,
    d_gain_ref,
    leave_ref,
    stay_ref,
    *,
    head_dim,
):
    width = query_ref.shape[1]
    half = head_dim // 2
    score_scale = head_dim ** (-0.5)
    sources = (
        (own_ref, own_place_ref[...] <= place_ref[...]),
        (other_ref, other_place_ref[...] <= place_ref[...]),
    )
    cosines, sines = cosine_ref[...], sine_ref[...]
    d_keys = [0.0, 0.0]
    d_values = [0.0, 0.0]
    d_gain = 0.0
    for start in range(0, width, head_dim):
        part = slice(start, start + head_dim)
        head = start // head_dim
        query = query_ref[:, part]
        d_mixing = times_transposed(d_attend_ref[...], out_ref[part, :]).astype(jnp.bfloat16)
        delta = jnp.sum(
            d_mixing.astype(jnp.float32) * mixing_ref[:, part], axis=-1, keepdims=True
        )
        d_rotated = 0.0
        for number, (both_ref, allowed) in enumerate(sources):
            keys = both_ref[:, :head_dim]
            scores = times_transposed(query, keys) * score_scale
            weights = jnp.where(allowed, jnp.exp(scores - log_ref[:, head : head + 1]), 0.0)
            d_weights = times_transposed(d_mixing, both_ref[:, head_dim:])
            d_scores = (weights * (d_weights - delta) * score_scale).astype(jnp.bfloat16)
            d_rotated = d_rotated + product(d_scores, keys)
            d_keys[number] = d_keys[number] + transposed_times(d_scores, query)
            d_values[number] = d_values[number] + transposed_times(
                weights.astype(jnp.bfloat16), d_mixing
            )
        first, second = d_rotated[:, :half], d_rotated[:, half:]
        turned = jnp.concatenate(
            [first * cosines + second * sines, second * cosines - first * sines], axis=-1
        )
        d_query, d_gain_rows = norm_back(raw_ref[:, part], gain_ref[0:1, :], turned)
        d_query_ref[:, part] = d_query.astype(jnp.bfloat16)
        d_gain = d_gain + jnp.sum(d_gain_rows, axis=0, keepdims=True)
    d_gain_ref[...] = d_gain
    stay_ref[:, :head_dim] = d_keys[0]
    stay_ref[:, head_dim:] = d_values[0]
    leave_ref[:, :head_dim] = d_keys[1].astype(jnp.bfloat16)
    leave_ref[:, head_dim:] = d_values[1].astype(jnp.bfloat16)


def keys_back_body(
    stay_ref, back_ref, raw_ref, cosine_ref, sine_ref, gain_ref, d_both_ref, d_gain_ref
):
    head_dim = raw_ref.shape[1]
    half = head_dim // 2
    d_both = stay_ref[...] + back_ref[...].astype(jnp.float32)
    cosines, sines = cosine_ref[...], sine_ref[...]
    first, second = d_both[:, :half], d_both[:, half:head_dim]
    turned = jnp.concatenate(
        [first * cosines + second * sines, second * cosines - first * sines], axis=-1
    )
    d_keys, d_gain_rows = norm_back(raw_ref[...], gain_ref[1:2, :], turned)
    d_both_ref[:, :head_dim] = d_keys.astype(jnp.bfloat16)
    d_both_ref[:, head_dim:] = d_both[:, head_dim:].astype(jnp.bfloat16)
    d_gain_ref[...] = jnp.sum(d_gain_rows, axis=0, keepdims=True)


def assemble(pieces, moves, table, rows):
    width = pieces[0].shape[1]

    def body(table_ref, *refs):
        piece_refs = refs[: len(pieces)]
        out_refs = refs[len(pieces) : len(pieces) + len(rows)]
        sems = refs[-1]
        started = []
        for number, (piece, source, count, out, step, offset, entry) in enumerate(moves):
            start = pl.multiple_of(table_ref[entry] * step + offset, 16)
            copy = pltpu.make_async_copy(
                piece_refs[piece].at[pl.ds(source, count)],
                out_refs[out].at[pl.ds(start, count)],
                sems.at[number],
            )
            copy.start()
            started.append(copy)
        for copy in started:
            copy.wait()

    anywhere = pl.BlockSpec(memory_space=pl.ANY)
    return pl.pallas_call(
        body,
        out_shape=[jax.ShapeDtypeStruct((count, width), pieces[0].dtype) for count in rows],
        in_specs=[pl.BlockSpec(memory_space=pltpu.SMEM)] + [anywhere] * len(pieces),
        out_specs=[pl.BlockSpec(memory_space=pltpu.VMEM)] * len(rows),
        scratch_shapes=[pltpu.SemaphoreType.DMA((len(moves),))],
        name="assemble",
    )(table, *pieces)


class Links:
    def __init__(self, fsdp_size):
        self.size = fsdp_size
        self.bits = fsdp_size.bit_length() - 1
        self.deep = fsdp_size // 4
        self.chips = fsdp_size // 2
        self.ring = self.chips == 8
        self.index = lax.axis_index("fsdp")
        self.side = lax.axis_index("ctx")

    def across(self, array, bit):
        return lax.ppermute(array, "fsdp", [(i, i ^ (1 << bit)) for i in range(self.size)])

    def to_side(self, array):
        return lax.ppermute(array, "ctx", [(0, 1), (1, 0)])

    def by_side(self, here, there):
        return jnp.where(self.side == 0, here, there)

    def device_at(self, place, core):
        column = place // self.deep
        level = place % self.deep
        level = level + column * (self.deep - 1 - 2 * level)
        return level * 4 + column * 2 + core

    def place(self):
        column = (self.index // 2) % 2
        level = self.index // 4
        return level + column * (self.chips - 1 - 2 * level)

    def turned(self, array, step):
        pairs = [
            (
                self.device_at(place, core),
                self.device_at((place + step) % self.chips, core),
            )
            for place in range(self.chips)
            for core in range(2)
        ]
        return lax.ppermute(array, "fsdp", pairs)

    def order(self, shard):
        relative = shard ^ self.index
        found = relative * 0
        for bit in range(self.bits):
            found = found * 2 + ((relative >> bit) & 1)
        return found

    def gather(self, mats, relative, far_step):
        counts = [mat.shape[0] for mat in mats]
        total = sum(counts)
        starts = [sum(counts[:number]) for number in range(len(mats))]
        (shard,) = assemble(
            mats,
            [
                (number, 0, count, 0, 0, start, 0)
                for number, (count, start) in enumerate(zip(counts, starts))
            ],
            jnp.zeros((1,), jnp.int32),
            [total],
        )
        far = self.chips // 2
        pieces = [(shard, 0)]
        ahead, behind = shard, shard
        for distance in range(1, far):
            ahead = self.turned(ahead, 1)
            behind = self.turned(behind, -1)
            pieces += [(ahead, -distance), (behind, distance)]
        last = ahead if far_step > 0 else behind
        pieces.append((self.turned(last, far_step), far))
        arrays, moves, entries = [], [], []
        for other in range(2):
            for array, distance in pieces:
                owner = self.device_at(
                    (self.place() + distance) % self.chips, (self.index % 2) ^ other
                )
                number = len(arrays)
                arrays.append(self.across(array, 0) if other else array)
                entries.append(self.order(owner) if relative else owner)
                moves += [
                    (number, start, count, out, count, 0, number)
                    for out, (start, count) in enumerate(zip(starts, counts))
                ]
        table = jnp.stack(entries).astype(jnp.int32)
        return assemble(arrays, moves, table, [count * self.size for count in counts])

    def split(self, array, bit, relative):
        if relative:
            half = array.shape[0] // 2
            return array[:half], array[half:]
        own = (self.index >> bit) & 1
        axis = array.ndim - 3
        return (
            lax.dynamic_index_in_dim(array, own, axis, keepdims=False),
            lax.dynamic_index_in_dim(array, 1 - own, axis, keepdims=False),
        )

    def fold(self, terms, first_bit, relative, gains=None):
        for bit in range(first_bit, self.bits):
            parts = [self.split(term, bit, relative) for term in terms]
            leaving = total_of([part[1] for part in parts]).astype(jnp.bfloat16)
            if gains is None:
                received = self.across(leaving, bit)
            else:
                message, gains = self.loaded(leaving, gains)
                received, more = self.unloaded(self.across(message, bit), leaving)
                gains = gains + more
            terms = [part[0] for part in parts] + [received]
        total = total_of(terms).astype(jnp.bfloat16)
        return total if gains is None else (total, gains)

    def loaded(self, rows, gains):
        main = lax.reduce_precision(gains, 8, 7)
        rest = lax.reduce_precision(gains - main, 8, 7)
        width = rows.shape[-1]
        both = jnp.concatenate([main, rest], axis=0).astype(jnp.bfloat16)
        return jnp.concatenate([rows.reshape(-1, width), both], axis=0), main + rest

    def unloaded(self, message, rows):
        count = rows.size // rows.shape[-1]
        main, rest = jnp.split(message[count:].astype(jnp.float32), 2, axis=0)
        return message[:count].reshape(rows.shape), main + rest

    def blocks(self, array, relative):
        if relative:
            return array
        return array.reshape((2,) * self.bits + (-1, array.shape[-1]))


def total_of(terms):
    total = terms[0].astype(jnp.float32)
    for term in terms[1:]:
        total = total + term.astype(jnp.float32)
    return total


def per_device(
    block_in,
    positions,
    norm_gains,
    qk_gains,
    mat_query,
    mat_keyval,
    mat_out,
    mat_gate,
    mat_up,
    mat_down,
    cotangent,
    *,
    fsdp_size,
):
    stream = block_in[0].astype(jnp.float32)
    places = positions[0]
    row_count = stream.shape[0]
    head_dim = qk_gains.shape[1]
    links = Links(fsdp_size)
    other_places = links.to_side(positions)[0]
    relative = links.ring
    if links.ring:
        full_query, full_keyval, full_out = links.gather((mat_query, mat_keyval, mat_out), False, -1)
        full_gate, full_up = links.gather((mat_gate, mat_up), True, 1)
        (full_down,) = links.gather((mat_down,), True, -1)
    else:
        full_query, full_keyval, full_out, full_gate, full_up, full_down = [
            lax.all_gather(mat, "fsdp", axis=0, tiled=True)
            for mat in (mat_query, mat_keyval, mat_out, mat_gate, mat_up, mat_down)
        ]
    head_count = full_query.shape[0] // head_dim
    normed_in = rms_norm(stream, norm_gains[0]).astype(jnp.bfloat16)
    queries = times_transposed(normed_in, full_query)
    key_values = times_transposed(normed_in, full_keyval)
    key_raw = key_values[:, :head_dim]
    cosines, sine_table = rope_tables(places, head_dim)
    split_queries = queries.reshape(row_count, head_count, head_dim)
    query_rot = (
        rotate(
            rms_norm(split_queries, qk_gains[0]), cosines[:, None, :], sine_table[:, None, :]
        )
        .astype(jnp.bfloat16)
        .reshape(queries.shape)
    )
    key_rot = rotate(rms_norm(key_raw, qk_gains[1]), cosines, sine_table).astype(jnp.bfloat16)
    value_rows = key_values[:, head_dim:].astype(jnp.bfloat16)
    both_b = jnp.concatenate([key_rot, value_rows], axis=1)
    other_both = links.to_side(both_b)
    pairs = (both_b, other_both, places[:, None], places[None, :], other_places[None, :])
    like = functools.partial(jax.ShapeDtypeStruct, dtype=jnp.float32)
    mixing, mixing_b, log_total, attend_out, resid, normed_mid = pl.pallas_call(
        functools.partial(attend_body, head_dim=head_dim),
        out_shape=[
            like(queries.shape),
            jax.ShapeDtypeStruct(queries.shape, jnp.bfloat16),
            like((row_count, head_count)),
            like(stream.shape),
            like(stream.shape),
            jax.ShapeDtypeStruct(stream.shape, jnp.bfloat16),
        ],
        name="attend",
    )(query_rot, *pairs, full_out, block_in[0], norm_gains)
    gate_proj = times_transposed(normed_mid, full_gate)
    up_proj = times_transposed(normed_mid, full_up)
    hidden = gelu_gate(gate_proj, up_proj).astype(jnp.bfloat16)
    ffn_out = product(hidden, full_down)
    block_out = (resid + rms_norm(ffn_out, norm_gains[3])).astype(jnp.bfloat16)
    cot_full = cotangent[0].astype(jnp.float32)
    unused, ffn_back = jax.vjp(rms_norm, ffn_out, norm_gains[3])
    d_ffn, d_gain_three = ffn_back(cot_full)
    d_ffn_b = d_ffn.astype(jnp.bfloat16)
    d_hidden = times_transposed(d_ffn_b, full_down)

    def over_cores(rows, columns):
        if relative:
            half = rows.shape[1] // 2
            leaving = transposed_times(rows[:, half:], columns).astype(jnp.bfloat16)
            staying = transposed_times(rows[:, :half], columns).astype(jnp.bfloat16)
        else:
            product_b = transposed_times(rows, columns).astype(jnp.bfloat16)
            staying, leaving = links.split(links.blocks(product_b, relative), 0, relative)
        return [staying, links.across(leaving, 0)]

    def both_sides(total_b):
        return total_b.astype(jnp.float32) + links.to_side(total_b).astype(jnp.float32)

    shard_down = both_sides(links.fold(over_cores(hidden, d_ffn_b), 1, relative))
    unused, gate_back = jax.vjp(gelu_gate, gate_proj, up_proj)
    d_gate, d_up = gate_back(d_hidden)
    d_gate_b = d_gate.astype(jnp.bfloat16)
    d_up_b = d_up.astype(jnp.bfloat16)
    d_first = links.by_side(d_gate_b, d_up_b)
    d_second = links.by_side(d_up_b, d_gate_b)
    second_sum = total_of(over_cores(d_second, normed_mid)).astype(jnp.bfloat16)
    first_terms = [links.to_side(second_sum)] + over_cores(d_first, normed_mid)
    first_sum = links.fold(first_terms, 1, relative)
    second_sum = links.to_side(first_sum)
    shard_gate = links.by_side(first_sum, second_sum).astype(jnp.float32)
    shard_up = links.by_side(second_sum, first_sum).astype(jnp.float32)
    d_mid = product(d_gate_b, full_gate) + product(d_up_b, full_up)
    unused, mid_back = jax.vjp(rms_norm, resid, norm_gains[2])
    d_resid_mid, d_gain_two = mid_back(d_mid)
    d_resid = cot_full + d_resid_mid
    unused, attend_back = jax.vjp(rms_norm, attend_out, norm_gains[1])
    d_attend, d_gain_one = attend_back(d_resid)
    d_attend_b = d_attend.astype(jnp.bfloat16)

    def blocks_of(rows, columns):
        grad = transposed_times(rows, columns)
        return links.blocks(grad.astype(jnp.bfloat16), False)

    d_query_b, d_gain_query, key_leave, key_stay = pl.pallas_call(
        functools.partial(attend_back_body, head_dim=head_dim),
        out_shape=[
            jax.ShapeDtypeStruct(queries.shape, jnp.bfloat16),
            like((1, head_dim)),
            jax.ShapeDtypeStruct((row_count, 2 * head_dim), jnp.bfloat16),
            like((row_count, 2 * head_dim)),
        ],
        name="attend_back",
    )(
        d_attend_b,
        full_out,
        query_rot,
        *pairs,
        mixing,
        log_total,
        queries,
        cosines,
        sine_table,
        qk_gains,
    )
    key_back = links.to_side(key_leave)
    d_keyval_b, d_gain_key = pl.pallas_call(
        keys_back_body,
        out_shape=[
            jax.ShapeDtypeStruct(key_back.shape, jnp.bfloat16),
            like((1, head_dim)),
        ],
        name="keys_back",
    )(key_stay, key_back, key_raw, cosines, sine_table, qk_gains)
    heads_grads = jnp.concatenate(
        [blocks_of(mixing_b, d_attend_b), blocks_of(d_query_b, normed_in)],
        axis=-2,
    )
    heads_grads = both_sides(links.fold([heads_grads], 0, False))
    shard_out = heads_grads[: mat_out.shape[0]]
    shard_query = heads_grads[mat_out.shape[0] :]
    d_in = product(d_query_b, full_query) + product(d_keyval_b, full_keyval)
    unused, in_back = jax.vjp(rms_norm, stream, norm_gains[0])
    d_stream, d_gain_zero = in_back(d_in)
    grad_input = d_resid + d_stream
    gains = jnp.concatenate(
        [d_gain_zero, d_gain_one, d_gain_two, d_gain_three, d_gain_query[0], d_gain_key[0]]
    )
    gain_rows = -(-gains.size // stream.shape[1])
    gain_rows = gain_rows + (-gain_rows) % 8
    gains = jnp.pad(gains, (0, gain_rows * stream.shape[1] - gains.size)).reshape(gain_rows, -1)
    keyval_total, gains = links.fold([blocks_of(d_keyval_b, normed_in)], 0, False, gains)
    message, gains = links.loaded(keyval_total, gains)
    received, more = links.unloaded(links.to_side(message), keyval_total)
    shard_keyval = keyval_total.astype(jnp.float32) + received.astype(
        jnp.float32
    )
    gains = (gains + more).reshape(-1)
    grad_norms = gains[: norm_gains.size].reshape(norm_gains.shape)
    grad_qk = gains[norm_gains.size : norm_gains.size + qk_gains.size].reshape(qk_gains.shape)
    return (
        block_out[None],
        grad_input[None],
        shard_query,
        shard_keyval,
        shard_out,
        shard_gate,
        shard_up,
        shard_down,
        grad_norms,
        grad_qk,
    )


def solution(mesh):
    return jax.shard_map(
        functools.partial(per_device, fsdp_size=mesh.shape["fsdp"]),
        mesh=mesh,
        in_specs=(
            P("fsdp", "ctx", None),
            P("fsdp", "ctx"),
            P(),
            P(),
            P("fsdp", None),
            P("fsdp", None),
            P("fsdp", None),
            P("fsdp", None),
            P("fsdp", None),
            P("fsdp", None),
            P("fsdp", "ctx", None),
        ),
        out_specs=(
            P("fsdp", "ctx", None),
            P("fsdp", "ctx", None),
            P("fsdp", None),
            P("fsdp", None),
            P("fsdp", None),
            P("fsdp", None),
            P("fsdp", None),
            P("fsdp", None),
            P(),
            P(),
        ),
        check_vma=False,
    )
```

```python
import functools
import math

import jax
import jax.numpy as jnp
from jax import lax
from jax.experimental import pallas as pl
from jax.experimental.pallas import tpu as pltpu
from jax.sharding import PartitionSpec as P


EPS = 1e-06
ROPE_BASE = 1000000.0
NEG_FILL = -1e30


def rms_norm(vector, gains):
    return vector * lax.rsqrt(jnp.mean(vector * vector, axis=-1, keepdims=True) + EPS) * gains


def rope_tables(places, width):
    half_width = width // 2
    frequency = jnp.exp(
        jnp.arange(half_width, dtype=jnp.float32) * (-2.0 * math.log(ROPE_BASE) / width)
    )
    angles = places.astype(jnp.float32)[:, None] * frequency[None, :]
    return (jnp.cos(angles), jnp.sin(angles))


def rotate(vector, cosines, sine_table):
    half_width = vector.shape[-1] // 2
    first_half = vector[..., :half_width]
    second_half = vector[..., half_width:]
    return jnp.concatenate(
        [
            first_half * cosines - second_half * sine_table,
            second_half * cosines + first_half * sine_table,
        ],
        axis=-1,
    )


def product(left, right):
    return jnp.dot(left, right, preferred_element_type=jnp.float32)


def times_transposed(left, right):
    return lax.dot_general(
        left, right, (((1,), (1,)), ((), ())), preferred_element_type=jnp.float32
    )


def transposed_times(left, right):
    return lax.dot_general(
        left, right, (((0,), (0,)), ((), ())), preferred_element_type=jnp.float32
    )


def gelu_gate(gate_proj, up_proj):
    return jax.nn.gelu(gate_proj, approximate=True) * up_proj


def norm_back(vector, gains, cot):
    inverse = lax.rsqrt(jnp.mean(vector * vector, axis=-1, keepdims=True) + EPS)
    unit = vector * inverse
    scaled = cot * gains
    d_vector = inverse * (scaled - unit * jnp.mean(scaled * unit, axis=-1, keepdims=True))
    return d_vector, cot * unit


def attend_body(
    query_ref,
    own_ref,
    other_ref,
    place_ref,
    own_place_ref,
    other_place_ref,
    out_ref,
    stream_ref,
    gain_ref,
    mixing_ref,
    mixing_b_ref,
    log_ref,
    attend_ref,
    resid_ref,
    mid_ref,
    *,
    head_dim,
):
    rows, width = query_ref.shape
    score_scale = head_dim ** (-0.5)
    sources = (
        (own_ref, own_place_ref[...] <= place_ref[...]),
        (other_ref, other_place_ref[...] <= place_ref[...]),
    )
    for start in range(0, width, head_dim):
        query = query_ref[:, start : start + head_dim]
        scores = [
            jnp.where(
                allowed, times_transposed(query, both_ref[:, :head_dim]) * score_scale, NEG_FILL
            )
            for both_ref, allowed in sources
        ]
        best = jnp.maximum(
            jnp.max(scores[0], axis=-1, keepdims=True), jnp.max(scores[1], axis=-1, keepdims=True)
        )
        total = jnp.zeros((rows, 1), jnp.float32)
        weighted = jnp.zeros((rows, head_dim), jnp.float32)
        for (both_ref, allowed), score in zip(sources, scores):
            weights = jnp.where(allowed, jnp.exp(score - best), 0.0)
            total = total + jnp.sum(weights, axis=-1, keepdims=True)
            weighted = weighted + product(weights.astype(jnp.bfloat16), both_ref[:, head_dim:])
        mixing = weighted / total
        mixing_ref[:, start : start + head_dim] = mixing
        mixing_b_ref[:, start : start + head_dim] = mixing.astype(jnp.bfloat16)
        head = start // head_dim
        log_ref[:, head : head + 1] = best + jnp.log(total)
    attend = product(mixing_b_ref[...], out_ref[...])
    attend_ref[...] = attend
    resid = stream_ref[...].astype(jnp.float32) + rms_norm(attend, gain_ref[1:2, :])
    resid_ref[...] = resid
    mid_ref[...] = rms_norm(resid, gain_ref[2:3, :]).astype(jnp.bfloat16)


def attend_back_body(
    d_attend_ref,
    out_ref,
    query_ref,
    own_ref,
    other_ref,
    place_ref,
    own_place_ref,
    other_place_ref,
    mixing_ref,
    log_ref,
    raw_ref,
    cosine_ref,
    sine_ref,
    gain_ref,
    d_query_ref,
    d_gain_ref,
    leave_ref,
    stay_ref,
    *,
    head_dim,
):
    width = query_ref.shape[1]
    half = head_dim // 2
    score_scale = head_dim ** (-0.5)
    sources = (
        (own_ref, own_place_ref[...] <= place_ref[...]),
        (other_ref, other_place_ref[...] <= place_ref[...]),
    )
    cosines, sines = cosine_ref[...], sine_ref[...]
    d_keys = [0.0, 0.0]
    d_values = [0.0, 0.0]
    d_gain = 0.0
    for start in range(0, width, head_dim):
        part = slice(start, start + head_dim)
        head = start // head_dim
        query = query_ref[:, part]
        d_mixing = times_transposed(d_attend_ref[...], out_ref[part, :]).astype(jnp.bfloat16)
        delta = jnp.sum(
            d_mixing.astype(jnp.float32) * mixing_ref[:, part], axis=-1, keepdims=True
        )
        d_rotated = 0.0
        for number, (both_ref, allowed) in enumerate(sources):
            keys = both_ref[:, :head_dim]
            scores = times_transposed(query, keys) * score_scale
            weights = jnp.where(allowed, jnp.exp(scores - log_ref[:, head : head + 1]), 0.0)
            d_weights = times_transposed(d_mixing, both_ref[:, head_dim:])
            d_scores = (weights * (d_weights - delta) * score_scale).astype(jnp.bfloat16)
            d_rotated = d_rotated + product(d_scores, keys)
            d_keys[number] = d_keys[number] + transposed_times(d_scores, query)
            d_values[number] = d_values[number] + transposed_times(
                weights.astype(jnp.bfloat16), d_mixing
            )
        first, second = d_rotated[:, :half], d_rotated[:, half:]
        turned = jnp.concatenate(
            [first * cosines + second * sines, second * cosines - first * sines], axis=-1
        )
        d_query, d_gain_rows = norm_back(raw_ref[:, part], gain_ref[0:1, :], turned)
        d_query_ref[:, part] = d_query.astype(jnp.bfloat16)
        d_gain = d_gain + jnp.sum(d_gain_rows, axis=0, keepdims=True)
    d_gain_ref[...] = d_gain
    stay_ref[:, :head_dim] = d_keys[0]
    stay_ref[:, head_dim:] = d_values[0]
    leave_ref[:, :head_dim] = d_keys[1].astype(jnp.bfloat16)
    leave_ref[:, head_dim:] = d_values[1].astype(jnp.bfloat16)


def keys_back_body(
    stay_ref, back_ref, raw_ref, cosine_ref, sine_ref, gain_ref, d_both_ref, d_gain_ref
):
    head_dim = raw_ref.shape[1]
    half = head_dim // 2
    d_both = stay_ref[...] + back_ref[...].astype(jnp.float32)
    cosines, sines = cosine_ref[...], sine_ref[...]
    first, second = d_both[:, :half], d_both[:, half:head_dim]
    turned = jnp.concatenate(
        [first * cosines + second * sines, second * cosines - first * sines], axis=-1
    )
    d_keys, d_gain_rows = norm_back(raw_ref[...], gain_ref[1:2, :], turned)
    d_both_ref[:, :head_dim] = d_keys.astype(jnp.bfloat16)
    d_both_ref[:, head_dim:] = d_both[:, head_dim:].astype(jnp.bfloat16)
    d_gain_ref[...] = jnp.sum(d_gain_rows, axis=0, keepdims=True)


def start_moves(piece_refs, out_refs, table_ref, sems, moves):
    started = []
    for number, (piece, source, count, out, step, offset, entry) in enumerate(moves):
        start = pl.multiple_of(table_ref[entry] * step + offset, 16)
        copy = pltpu.make_async_copy(
            piece_refs[piece].at[pl.ds(source, count)],
            out_refs[out].at[pl.ds(start, count)],
            sems.at[number],
        )
        copy.start()
        started.append(copy)
    return started


def gelu_back(gate, up, d_hidden):
    root = math.sqrt(2.0 / math.pi)
    bend = jnp.tanh(root * (gate + 0.044715 * gate * gate * gate))
    slope = 0.5 * (1.0 + bend) + 0.5 * gate * (1.0 - bend * bend) * root * (
        1.0 + 3.0 * 0.044715 * gate * gate
    )
    return d_hidden * up * slope, d_hidden * (0.5 * gate * (1.0 + bend))


def wide_body(
    table_ref,
    side_ref,
    mid_ref,
    resid_ref,
    attend_ref,
    cot_ref,
    gain_ref,
    *refs,
    moves,
    blocks,
):
    count = len(refs) - 14
    piece_refs = refs[:count]
    block_out_ref, hidden_ref, d_ffn_ref, d_first_ref, d_second_ref = refs[count : count + 5]
    d_resid_ref, d_attend_ref, d_gain_ref = refs[count + 5 : count + 8]
    weights = refs[count + 8 : count + 11]
    gate_ref, up_ref, sems = refs[count + 11 :]
    started = start_moves(piece_refs, weights, table_ref, sems, moves)
    for copy, move in zip(started, moves):
        if move[3] < 2:
            copy.wait()
    mid = mid_ref[...]
    span = gate_ref.shape[1] // blocks
    parts = [slice(number * span, (number + 1) * span) for number in range(blocks)]
    for part in parts:
        gate = times_transposed(mid, weights[0][part, :])
        up = times_transposed(mid, weights[1][part, :])
        gate_ref[:, part] = gate
        up_ref[:, part] = up
        hidden_ref[:, part] = gelu_gate(gate, up).astype(jnp.bfloat16)
    for copy, move in zip(started, moves):
        if move[3] == 2:
            copy.wait()
    ffn_out = product(hidden_ref[...], weights[2][...])
    resid = resid_ref[...]
    block_out_ref[...] = (resid + rms_norm(ffn_out, gain_ref[3:4, :])).astype(jnp.bfloat16)
    cot = cot_ref[...].astype(jnp.float32)
    d_ffn, rows_three = norm_back(ffn_out, gain_ref[3:4, :], cot)
    d_ffn_ref[...] = d_ffn.astype(jnp.bfloat16)
    first_is_gate = side_ref[0] == 0
    d_mid = jnp.zeros(resid.shape, jnp.float32)
    for part in parts:
        d_hidden = times_transposed(d_ffn_ref[...], weights[2][part, :])
        d_gate, d_up = gelu_back(gate_ref[:, part], up_ref[:, part], d_hidden)
        d_first_ref[:, part] = jnp.where(first_is_gate, d_gate, d_up).astype(jnp.bfloat16)
        d_second_ref[:, part] = jnp.where(first_is_gate, d_up, d_gate).astype(jnp.bfloat16)
        d_mid = d_mid + product(d_gate.astype(jnp.bfloat16), weights[0][part, :])
        d_mid = d_mid + product(d_up.astype(jnp.bfloat16), weights[1][part, :])
    d_resid_mid, rows_two = norm_back(resid, gain_ref[2:3, :], d_mid)
    d_resid = cot + d_resid_mid
    d_resid_ref[...] = d_resid
    d_attend, rows_one = norm_back(attend_ref[...], gain_ref[1:2, :], d_resid)
    d_attend_ref[...] = d_attend.astype(jnp.bfloat16)
    for number, rows in enumerate((rows_one, rows_two, rows_three)):
        d_gain_ref[number : number + 1, :] = jnp.sum(rows, axis=0, keepdims=True)


def assemble(pieces, moves, table, rows):
    width = pieces[0].shape[1]

    def body(table_ref, *refs):
        piece_refs = refs[: len(pieces)]
        out_refs = refs[len(pieces) : len(pieces) + len(rows)]
        sems = refs[-1]
        for copy in start_moves(piece_refs, out_refs, table_ref, sems, moves):
            copy.wait()

    anywhere = pl.BlockSpec(memory_space=pl.ANY)
    return pl.pallas_call(
        body,
        out_shape=[jax.ShapeDtypeStruct((count, width), pieces[0].dtype) for count in rows],
        in_specs=[pl.BlockSpec(memory_space=pltpu.SMEM)] + [anywhere] * len(pieces),
        out_specs=[pl.BlockSpec(memory_space=pltpu.VMEM)] * len(rows),
        scratch_shapes=[pltpu.SemaphoreType.DMA((len(moves),))],
        name="assemble",
    )(table, *pieces)


class Links:
    def __init__(self, fsdp_size):
        self.size = fsdp_size
        self.bits = fsdp_size.bit_length() - 1
        self.deep = fsdp_size // 4
        self.chips = fsdp_size // 2
        self.ring = self.chips == 8
        self.index = lax.axis_index("fsdp")
        self.side = lax.axis_index("ctx")

    def across(self, array, bit):
        return lax.ppermute(array, "fsdp", [(i, i ^ (1 << bit)) for i in range(self.size)])

    def to_side(self, array):
        return lax.ppermute(array, "ctx", [(0, 1), (1, 0)])

    def by_side(self, here, there):
        return jnp.where(self.side == 0, here, there)

    def device_at(self, place, core):
        column = place // self.deep
        level = place % self.deep
        level = level + column * (self.deep - 1 - 2 * level)
        return level * 4 + column * 2 + core

    def place(self):
        column = (self.index // 2) % 2
        level = self.index // 4
        return level + column * (self.chips - 1 - 2 * level)

    def turned(self, array, step):
        pairs = [
            (
                self.device_at(place, core),
                self.device_at((place + step) % self.chips, core),
            )
            for place in range(self.chips)
            for core in range(2)
        ]
        return lax.ppermute(array, "fsdp", pairs)

    def order(self, shard):
        relative = shard ^ self.index
        found = relative * 0
        for bit in range(self.bits):
            found = found * 2 + ((relative >> bit) & 1)
        return found

    def gather(self, mats, relative, far_step):
        counts = [mat.shape[0] for mat in mats]
        total = sum(counts)
        starts = [sum(counts[:number]) for number in range(len(mats))]
        (shard,) = assemble(
            mats,
            [
                (number, 0, count, 0, 0, start, 0)
                for number, (count, start) in enumerate(zip(counts, starts))
            ],
            jnp.zeros((1,), jnp.int32),
            [total],
        )
        far = self.chips // 2
        pieces = [(shard, 0)]
        ahead, behind = shard, shard
        for distance in range(1, far):
            ahead = self.turned(ahead, 1)
            behind = self.turned(behind, -1)
            pieces += [(ahead, -distance), (behind, distance)]
        last = ahead if far_step > 0 else behind
        pieces.append((self.turned(last, far_step), far))
        arrays, moves, entries = [], [], []
        for other in range(2):
            for array, distance in pieces:
                owner = self.device_at(
                    (self.place() + distance) % self.chips, (self.index % 2) ^ other
                )
                number = len(arrays)
                arrays.append(self.across(array, 0) if other else array)
                entries.append(self.order(owner) if relative else owner)
                moves += [
                    (number, start, count, out, count, 0, number)
                    for out, (start, count) in enumerate(zip(starts, counts))
                ]
        table = jnp.stack(entries).astype(jnp.int32)
        return arrays, moves, table, [count * self.size for count in counts]

    def split(self, array, bit, relative):
        if relative:
            half = array.shape[0] // 2
            return array[:half], array[half:]
        own = (self.index >> bit) & 1
        axis = array.ndim - 3
        return (
            lax.dynamic_index_in_dim(array, own, axis, keepdims=False),
            lax.dynamic_index_in_dim(array, 1 - own, axis, keepdims=False),
        )

    def fold(self, terms, first_bit, relative, gains=None):
        for bit in range(first_bit, self.bits):
            parts = [self.split(term, bit, relative) for term in terms]
            leaving = total_of([part[1] for part in parts]).astype(jnp.bfloat16)
            if gains is None:
                received = self.across(leaving, bit)
            else:
                message, gains = self.loaded(leaving, gains)
                received, more = self.unloaded(self.across(message, bit), leaving)
                gains = gains + more
            terms = [part[0] for part in parts] + [received]
        total = total_of(terms).astype(jnp.bfloat16)
        return total if gains is None else (total, gains)

    def loaded(self, rows, gains):
        main = lax.reduce_precision(gains, 8, 7)
        rest = lax.reduce_precision(gains - main, 8, 7)
        width = rows.shape[-1]
        both = jnp.concatenate([main, rest], axis=0).astype(jnp.bfloat16)
        return jnp.concatenate([rows.reshape(-1, width), both], axis=0), main + rest

    def unloaded(self, message, rows):
        count = rows.size // rows.shape[-1]
        main, rest = jnp.split(message[count:].astype(jnp.float32), 2, axis=0)
        return message[:count].reshape(rows.shape), main + rest

    def blocks(self, array, relative):
        if relative:
            return array
        return array.reshape((2,) * self.bits + (-1, array.shape[-1]))


def total_of(terms):
    total = terms[0].astype(jnp.float32)
    for term in terms[1:]:
        total = total + term.astype(jnp.float32)
    return total


def per_device(
    block_in,
    positions,
    norm_gains,
    qk_gains,
    mat_query,
    mat_keyval,
    mat_out,
    mat_gate,
    mat_up,
    mat_down,
    cotangent,
    *,
    fsdp_size,
):
    stream = block_in[0].astype(jnp.float32)
    places = positions[0]
    row_count = stream.shape[0]
    head_dim = qk_gains.shape[1]
    links = Links(fsdp_size)
    side = links.side
    other_places = links.to_side(positions)[0]
    relative = links.ring
    if links.ring:
        heads_parts = links.gather((mat_query, mat_keyval, mat_out), False, -1)
        full_query, full_keyval, full_out = assemble(*heads_parts)
        arrays, moves, table, wide_rows = links.gather((mat_gate, mat_up), True, 1)
        more, more_moves, more_table, down_rows = links.gather((mat_down,), True, -1)
        moves = moves + [
            (piece + len(arrays), source, count, out + 2, step, offset, entry + table.size)
            for piece, source, count, out, step, offset, entry in more_moves
        ]
        arrays = arrays + more
        table = jnp.concatenate([table, more_table])
        wide_rows = wide_rows + down_rows
    else:
        full_query, full_keyval, full_out, *arrays = [
            lax.all_gather(mat, "fsdp", axis=0, tiled=True)
            for mat in (mat_query, mat_keyval, mat_out, mat_gate, mat_up, mat_down)
        ]
        wide_rows = [array.shape[0] for array in arrays]
        moves = [(number, 0, count, number, 0, 0, 0) for number, count in enumerate(wide_rows)]
        table = jnp.zeros((1,), jnp.int32)
    head_count = full_query.shape[0] // head_dim
    normed_in = rms_norm(stream, norm_gains[0]).astype(jnp.bfloat16)
    queries = times_transposed(normed_in, full_query)
    key_values = times_transposed(normed_in, full_keyval)
    key_raw = key_values[:, :head_dim]
    cosines, sine_table = rope_tables(places, head_dim)
    split_queries = queries.reshape(row_count, head_count, head_dim)
    query_rot = (
        rotate(
            rms_norm(split_queries, qk_gains[0]), cosines[:, None, :], sine_table[:, None, :]
        )
        .astype(jnp.bfloat16)
        .reshape(queries.shape)
    )
    key_rot = rotate(rms_norm(key_raw, qk_gains[1]), cosines, sine_table).astype(jnp.bfloat16)
    value_rows = key_values[:, head_dim:].astype(jnp.bfloat16)
    both_b = jnp.concatenate([key_rot, value_rows], axis=1)
    other_both = links.to_side(both_b)
    pairs = (both_b, other_both, places[:, None], places[None, :], other_places[None, :])
    like = functools.partial(jax.ShapeDtypeStruct, dtype=jnp.float32)
    mixing, mixing_b, log_total, attend_out, resid, normed_mid = pl.pallas_call(
        functools.partial(attend_body, head_dim=head_dim),
        out_shape=[
            like(queries.shape),
            jax.ShapeDtypeStruct(queries.shape, jnp.bfloat16),
            like((row_count, head_count)),
            like(stream.shape),
            like(stream.shape),
            jax.ShapeDtypeStruct(stream.shape, jnp.bfloat16),
        ],
        name="attend",
    )(query_rot, *pairs, full_out, block_in[0], norm_gains)
    half_float = functools.partial(jax.ShapeDtypeStruct, dtype=jnp.bfloat16)
    units = wide_rows[0]
    scalars = pl.BlockSpec(memory_space=pltpu.SMEM)
    near = pl.BlockSpec(memory_space=pltpu.VMEM)
    block_out, hidden, d_ffn_b, d_first, d_second, d_resid, d_attend_b, d_gains = (
        pl.pallas_call(
            functools.partial(wide_body, moves=moves, blocks=4),
            out_shape=[
                half_float(stream.shape),
                half_float((row_count, units)),
                half_float(stream.shape),
                half_float((row_count, units)),
                half_float((row_count, units)),
                like(stream.shape),
                half_float(stream.shape),
                like((3, stream.shape[1])),
            ],
            in_specs=[scalars] * 2
            + [near] * 5
            + [pl.BlockSpec(memory_space=pl.ANY)] * len(arrays),
            scratch_shapes=[pltpu.VMEM((rows, stream.shape[1]), jnp.bfloat16) for rows in wide_rows]
            + [pltpu.VMEM((row_count, units), jnp.float32)] * 2
            + [pltpu.SemaphoreType.DMA((len(moves),))],
            name="wide",
        )(
            table,
            side.reshape(1).astype(jnp.int32),
            normed_mid,
            resid,
            attend_out,
            cotangent[0],
            norm_gains,
            *arrays,
        )
    )

    def over_cores(rows, columns):
        if relative:
            half = rows.shape[1] // 2
            leaving = transposed_times(rows[:, half:], columns).astype(jnp.bfloat16)
            staying = transposed_times(rows[:, :half], columns).astype(jnp.bfloat16)
        else:
            product_b = transposed_times(rows, columns).astype(jnp.bfloat16)
            staying, leaving = links.split(links.blocks(product_b, relative), 0, relative)
        return [staying, links.across(leaving, 0)]

    def both_sides(total_b):
        received = links.to_side(total_b)
        return total_b.astype(jnp.float32) + received.astype(jnp.float32)

    shard_down = both_sides(links.fold(over_cores(hidden, d_ffn_b), 1, relative))
    second_terms = over_cores(d_second, normed_mid)
    second_sum = total_of(second_terms).astype(jnp.bfloat16)
    first_terms = [links.to_side(second_sum)] + over_cores(d_first, normed_mid)
    first_sum = links.fold(first_terms, 1, relative)
    second_sum = links.to_side(first_sum)
    shard_gate = links.by_side(first_sum, second_sum).astype(jnp.float32)
    shard_up = links.by_side(second_sum, first_sum).astype(jnp.float32)

    def blocks_of(rows, columns):
        grad = transposed_times(rows, columns)
        return links.blocks(grad.astype(jnp.bfloat16), False)

    d_query_b, d_gain_query, key_leave, key_stay = pl.pallas_call(
        functools.partial(attend_back_body, head_dim=head_dim),
        out_shape=[
            jax.ShapeDtypeStruct(queries.shape, jnp.bfloat16),
            like((1, head_dim)),
            jax.ShapeDtypeStruct((row_count, 2 * head_dim), jnp.bfloat16),
            like((row_count, 2 * head_dim)),
        ],
        name="attend_back",
    )(
        d_attend_b,
        full_out,
        query_rot,
        *pairs,
        mixing,
        log_total,
        queries,
        cosines,
        sine_table,
        qk_gains,
    )
    key_back = links.to_side(key_leave)
    d_keyval_b, d_gain_key = pl.pallas_call(
        keys_back_body,
        out_shape=[
            jax.ShapeDtypeStruct(key_back.shape, jnp.bfloat16),
            like((1, head_dim)),
        ],
        name="keys_back",
    )(key_stay, key_back, key_raw, cosines, sine_table, qk_gains)
    heads_grads = jnp.concatenate(
        [blocks_of(mixing_b, d_attend_b), blocks_of(d_query_b, normed_in)],
        axis=-2,
    )
    heads_grads = both_sides(links.fold([heads_grads], 0, False))
    shard_out = heads_grads[: mat_out.shape[0]]
    shard_query = heads_grads[mat_out.shape[0] :]
    d_in = product(d_query_b, full_query) + product(d_keyval_b, full_keyval)
    _, in_back = jax.vjp(rms_norm, stream, norm_gains[0])
    d_stream, d_gain_zero = in_back(d_in)
    grad_input = d_resid + d_stream
    gains = jnp.concatenate(
        [d_gain_zero, d_gains[0], d_gains[1], d_gains[2], d_gain_query[0], d_gain_key[0]]
    )
    gain_rows = -(-gains.size // stream.shape[1])
    gain_rows = gain_rows + (-gain_rows) % 8
    gains = jnp.pad(gains, (0, gain_rows * stream.shape[1] - gains.size)).reshape(gain_rows, -1)
    keyval_total, gains = links.fold([blocks_of(d_keyval_b, normed_in)], 0, False, gains)
    message, gains = links.loaded(keyval_total, gains)
    received, more = links.unloaded(links.to_side(message), keyval_total)
    shard_keyval = keyval_total.astype(jnp.float32) + received.astype(
        jnp.float32
    )
    gains = (gains + more).reshape(-1)
    grad_norms = gains[: norm_gains.size].reshape(norm_gains.shape)
    grad_qk = gains[norm_gains.size : norm_gains.size + qk_gains.size].reshape(qk_gains.shape)
    return (
        block_out[None],
        grad_input[None],
        shard_query,
        shard_keyval,
        shard_out,
        shard_gate,
        shard_up,
        shard_down,
        grad_norms,
        grad_qk,
    )


def solution(mesh):
    return jax.shard_map(
        functools.partial(per_device, fsdp_size=mesh.shape["fsdp"]),
        mesh=mesh,
        in_specs=(
            P("fsdp", "ctx", None),
            P("fsdp", "ctx"),
            P(),
            P(),
            P("fsdp", None),
            P("fsdp", None),
            P("fsdp", None),
            P("fsdp", None),
            P("fsdp", None),
            P("fsdp", None),
            P("fsdp", "ctx", None),
        ),
        out_specs=(
            P("fsdp", "ctx", None),
            P("fsdp", "ctx", None),
            P("fsdp", None),
            P("fsdp", None),
            P("fsdp", None),
            P("fsdp", None),
            P("fsdp", None),
            P("fsdp", None),
            P(),
            P(),
        ),
        check_vma=False,
    )
```
